32 devices in a mesh: batch: 1, seq: 32 (over z, y, x, core).
Axes of the slice: x: 2, y: 2, z: 4, core: 2. Of those that a mesh axis runs over, the one named last changes fastest.
Arguments:
- tokens: bfloat16 [304, 262144], P('batch', 'seq'), may hold values from -6 to 6
- norm_gain: float32 [2, 304], replicated, may hold values from 0.5 to 1.5
- in_weight: bfloat16 [2, 608, 304], replicated, may hold values from -0.3125 to 0.3125
- in_bias: float32 [2, 608], replicated, may hold values from -3 to 3
- out_weight: bfloat16 [2, 304, 608], replicated, may hold values from -0.25 to 0.25
- out_bias: float32 [2, 304], replicated, may hold values from -3 to 3
Outputs:
- mixed: bfloat16 [304, 262144], P('batch', 'seq')
The draws below stay inside these ranges and needn't reach their ends.
All inputs are finite; a program needn't handle non-finite values.
Results may differ from the reference program's by a relative error of at most 0.0056.
Values may be sent and summed in bfloat16 or wider, within the bound.
A program may use at most 64 MiB of HBM per device.

```python
import jax
import jax.numpy as jnp
from jax import lax

TRACK_CH = 16
TRACKS = 19
LENGTH = 262144
BLOCKS = 2
D = 304
HID = 608


def shard_levels(key, extent, split, smallest, largest):
    loudness, own = 1.0, jax.random.fold_in(key, 6)
    for axis_at, shards_of in split:
        heights = jnp.exp(jax.random.uniform(jax.random.fold_in(own, axis_at), (shards_of,), jnp.float32, smallest / len(split), largest / len(split)))
        loudness = loudness * jnp.repeat(heights, extent[axis_at] // shards_of).reshape([-1 if axis == axis_at else 1 for axis in range(len(extent))])
    return loudness


def normal_values(stream_key, extent, deviation, bound, split=(), kind=jnp.bfloat16):
    array = deviation * jax.random.normal(stream_key, extent, jnp.float32)
    if split:
        array = array * shard_levels(stream_key, extent, split, -0.22, 0.18)
    return jnp.clip(array, -bound, bound).astype(kind)


def setup_inputs(seed: int = 0, part: int = 0) -> dict:
    seeds = jax.random.split(jax.random.key(seed), 7)
    part_keys = jax.random.split(jax.random.fold_in(seeds[6], part), 7)
    tokens = normal_values(part_keys[0], (D, LENGTH), 1.0, 6.0, ((1, 32),))
    norm_gain = jnp.clip(jax.random.uniform(seeds[1], (BLOCKS, D), jnp.float32, 0.5, 1.5), 0.5, 1.5)
    in_weight = normal_values(seeds[2], (BLOCKS, HID, D), D ** -0.5, 0.3125)
    in_bias = normal_values(seeds[3], (BLOCKS, HID), 0.5, 3.0, (), jnp.float32)
    out_weight = normal_values(seeds[4], (BLOCKS, D, HID), HID ** -0.5, 0.25)
    out_bias = normal_values(seeds[5], (BLOCKS, D), 0.5, 3.0, (), jnp.float32)
    return dict(tokens=tokens, norm_gain=norm_gain, in_weight=in_weight, in_bias=in_bias, out_weight=out_weight, out_bias=out_bias)


def rotate(current):
    pieces = [current[0:TRACK_CH]]
    for track_no in range(1, TRACKS):
        offset = 2 ** (track_no - 1)
        one_track = current[track_no * TRACK_CH:(track_no + 1) * TRACK_CH]
        pieces.append(jnp.roll(one_track, offset, axis=1))
    return jnp.concatenate(pieces, 0)

def mix_rows(rotated, gain, in_weight, in_bias, out_weight, out_bias):
    as_float = rotated.astype(jnp.float32)
    mean_square = lax.optimization_barrier(jnp.mean(as_float * as_float, axis=0, keepdims=True))
    normed = (as_float * gain[:, None] * lax.rsqrt(mean_square + 1e-06)).astype(jnp.bfloat16)
    pre_act = jnp.dot(in_weight, normed, preferred_element_type=jnp.float32) + in_bias[:, None]
    active = jax.nn.gelu(pre_act, approximate=True).astype(jnp.bfloat16)
    summed = as_float + jnp.dot(out_weight, active, preferred_element_type=jnp.float32) + out_bias[:, None]
    return summed.astype(jnp.bfloat16)

def reference(tokens, norm_gain, in_weight, in_bias, out_weight, out_bias):
    current = tokens
    piece_count = 64
    piece_cols = LENGTH // piece_count
    for block_no in range(BLOCKS):
        rotated = rotate(current)
        stacked = rotated.reshape(D, piece_count, piece_cols).transpose(1, 0, 2)
        result = lax.map(lambda column_block: mix_rows(column_block, norm_gain[block_no], in_weight[block_no], in_bias[block_no], out_weight[block_no], out_bias[block_no]), stacked)
        current = result.transpose(1, 0, 2).reshape(D, LENGTH)
    return current
```

```python
import functools

import jax
import jax.numpy as jnp
from jax import lax
from jax.experimental import pallas as pl
from jax.experimental.pallas import tpu as pltpu
from jax.sharding import PartitionSpec as P

TRACK_CH = 16
TRACKS = 19
BLOCKS = 2
LANES = 128
CHUNK = 1024
LAG = 2
AHEAD = 1
WINDOW = 3
MESH = pl.DeviceIdType.MESH


class Plan:
    def __init__(self, count, rows, chunk, plane):
        self.count, self.rows, self.chunk = count, rows, chunk
        self.chunks = rows // chunk
        self.short = 0
        while self.short + 1 < TRACKS and 2**self.short < rows:
            self.short += 1
        self.near = (1 + self.short) * TRACK_CH
        self.distances = [2 ** (t - 1) // rows for t in range(1 + self.short, TRACKS)]
        self.far = len(self.distances)
        self.halo = max(2 ** (self.short - 1), LANES)
        self.pieces = []
        small = sum(1 for t in range(1, 1 + self.short) if 2 ** (t - 1) < LANES)
        self.pieces.append((TRACK_CH, small * TRACK_CH, LANES, LANES, self.chunks - 1, 0))
        for t in range(1 + small, 1 + self.short):
            offset = 2 ** (t - 1)
            width = min(offset, chunk)
            for part in range(offset // width):
                from_end = offset - part * width
                source = (rows - from_end) // chunk
                self.pieces.append((t * TRACK_CH, TRACK_CH, from_end, width, source, part))
        self.pieces.sort(key=lambda piece: (-piece[5], piece[2] if piece[3] < chunk else -piece[2]))
        big = [piece for piece in self.pieces if piece[1] * piece[3] >= TRACK_CH * chunk]
        self.pieces = big + [piece for piece in self.pieces if piece not in big]
        self.steps = [
            max(min(at, self.chunks - 1), self.chunks - 1 - piece[4]) for at, piece in enumerate(self.pieces)
        ]
        self.plane = plane
        self.relays = []
        if plane:
            last = plane - 1
            self.relays = [(0, last, 2, 0), (None, last, 3, 0), (1, last - 1, 0, 0), (1, last, 1, 1)]
        peers = []
        hops = [1] + self.distances
        for _, sender, relay, receiver in self.relays:
            hops += [(relay - sender) % count, (plane + receiver - relay) % count]
        for d in hops:
            for signed in (d, count - d):
                if signed % count and signed % count not in peers:
                    peers.append(signed % count)
        self.peers = peers


def rotated_tile(plan, ext, far, col):
    tile, halo = plan.chunk, plan.halo
    parts = []
    for t in range(1 + plan.short):
        rows = pl.ds(t * TRACK_CH, TRACK_CH)
        offset = 0 if t == 0 else 2 ** (t - 1)
        if offset % LANES == 0:
            start = pl.multiple_of(halo - offset + col, LANES)
            parts.append(ext[rows, pl.ds(start, tile)].astype(jnp.float32))
        else:
            start = pl.multiple_of(halo - LANES + col, LANES)
            window = ext[rows, pl.ds(start, tile + LANES)].astype(jnp.float32)
            parts.append(pltpu.roll(window, offset, 1)[:, LANES:])
    parts.append(far[:, pl.ds(pl.multiple_of(col, LANES), tile)].astype(jnp.float32))
    return jnp.concatenate(parts, 0)


def columns(row):
    return jnp.broadcast_to(row, (LANES, row.shape[1])).T


def across(column, width):
    return jnp.concatenate([column] * (width // LANES), 1)


def mix_tile(as_float, gain, in_weight, in_bias, out_weight, out_bias):
    mean_square = jnp.mean(as_float * as_float, axis=0, keepdims=True)
    normed = (as_float * gain * lax.rsqrt(mean_square + 1e-06)).astype(jnp.bfloat16)
    pre_act = jnp.dot(in_weight, normed, preferred_element_type=jnp.float32) + in_bias
    inner = pre_act * (0.7978845608028654 + 0.035677408136300125 * (pre_act * pre_act))
    half = 0.5 * pre_act
    active = (half + half * jnp.tanh(inner)).astype(jnp.bfloat16)
    summed = as_float + jnp.dot(out_weight, active, preferred_element_type=jnp.float32) + out_bias
    return summed.astype(jnp.bfloat16)


def kernel(plan, tokens, gain_in, w_in_in, b_in_in, w_out_in, b_out_in, out,
           gain_row, w_in_t, b_in_row, w_out, b_out_row, gain, w_in, b_in, b_out,
           relay_far, relay_halo, ext0, ext1, far0, far1, sent1,
           far_send, far_recv, halo_send, halo_recv,
           pass_send, pass_recv, pass_halo_send, pass_halo_recv, load_sem):
    me = lax.axis_index("seq")
    chunk, near, halo, rows = plan.chunk, plan.near, plan.halo, plan.rows
    exts, fars = (ext0, ext1), (far0, far1)

    loads = [
        pltpu.make_async_copy(source, target, load_sem.at[at])
        for at, (source, target) in enumerate((
            (gain_in, gain_row), (w_in_in, w_in_t), (b_in_in, b_in_row), (w_out_in, w_out), (b_out_in, b_out_row),
            (tokens.at[pl.ds(0, near), :], ext0.at[:, pl.ds(halo, rows)]),
        ))
    ]
    for load in loads:
        load.start()

    barrier = pltpu.get_barrier_semaphore()
    for peer in plan.peers:
        pl.semaphore_signal(barrier, inc=1, device_id={"seq": lax.rem(me + peer, plan.count)}, device_id_type=MESH)
    pl.semaphore_wait(barrier, len(plan.peers))

    place = lax.rem(me, plan.plane) if plan.plane else me

    def along(hop):
        return {"seq": lax.rem(me + hop + plan.count, plan.count)}

    def far_copy(block, index, number, relay=None):
        cols = pl.ds(pl.multiple_of(number * chunk, LANES), chunk)
        if block == 0:
            source = tokens.at[pl.ds(near + index * TRACK_CH, TRACK_CH), cols]
        else:
            source = sent1.at[pl.ds(index * TRACK_CH, TRACK_CH), cols]
        if relay is None:
            target = fars[block].at[pl.ds(index * TRACK_CH, TRACK_CH), cols]
            arrived, hop = far_recv.at[block, index, number], plan.distances[index]
        else:
            target, arrived, hop = relay_far.at[block, :, cols], pass_recv.at[block, number], relay[2] - relay[1]
        return pltpu.make_async_remote_copy(
            src_ref=source, dst_ref=target, send_sem=far_send.at[block, index, number], recv_sem=arrived,
            device_id=along(hop), device_id_type=MESH,
        )

    def far_pass(block, relay, number):
        index, _, at, receiver = relay
        cols = pl.ds(pl.multiple_of(number * chunk, LANES), chunk)
        return pltpu.make_async_remote_copy(
            src_ref=relay_far.at[block, :, cols],
            dst_ref=fars[block].at[pl.ds(index * TRACK_CH, TRACK_CH), cols],
            send_sem=pass_send.at[block, number],
            recv_sem=far_recv.at[block, index, number],
            device_id=along(plan.plane + receiver - at), device_id_type=MESH,
        )

    def halo_copy(block, number, relay=None):
        first, height, from_end, width, _, _ = plan.pieces[number]
        where = (pl.ds(first, height), pl.ds(halo - from_end, width))
        if block == 0:
            source = tokens.at[pl.ds(first, height), pl.ds(rows - from_end, width)]
        else:
            source = ext1.at[pl.ds(first, height), pl.ds(halo + rows - from_end, width)]
        if relay is None:
            target, arrived, hop = exts[block].at[where], halo_recv.at[block, number], 1
        else:
            target, arrived = relay_halo.at[(block, *where)], pass_halo_recv.at[block, number]
            hop = relay[2] - relay[1]
        return pltpu.make_async_remote_copy(
            src_ref=source, dst_ref=target, send_sem=halo_send.at[block, number], recv_sem=arrived,
            device_id=along(hop), device_id_type=MESH,
        )

    def halo_pass(block, relay, number):
        first, height, from_end, width, _, _ = plan.pieces[number]
        where = (pl.ds(first, height), pl.ds(halo - from_end, width))
        return pltpu.make_async_remote_copy(
            src_ref=relay_halo.at[(block, *where)],
            dst_ref=exts[block].at[where],
            send_sem=pass_halo_send.at[block, number],
            recv_sem=halo_recv.at[block, number],
            device_id=along(plan.plane + relay[3] - relay[2]), device_id_type=MESH,
        )

    def start(make, key, *args, direct=True, relayed=True):
        relays = [relay for relay in plan.relays if relay[0] == key]
        if relayed:
            for relay in relays:
                @pl.when(place == relay[1])
                def _(relay=relay):
                    make(*args, relay=relay).start()

        if direct and relays:
            own = place >= 0
            for relay in relays:
                own = own & (place != relay[1])

            @pl.when(own)
            def _():
                make(*args).start()
        elif direct:
            make(*args).start()

    def send(block, step, **kinds):
        for index in reversed(range(plan.far)):
            start(far_copy, index, block, index, plan.chunks - 1 - step, **kinds)
        for piece, at in enumerate(plan.steps):
            @pl.when(step == at)
            def _(piece=piece):
                start(halo_copy, None, block, piece, **kinds)

    def pass_far(block, number):
        for relay in plan.relays:
            if relay[0] is not None:
                @pl.when(place == relay[2])
                def _(relay=relay):
                    far_copy(block, relay[0], number, relay).wait_recv()
                    far_pass(block, relay, number).start()

    def pass_halo(block, piece):
        for relay in plan.relays:
            if relay[0] is None:
                @pl.when(place == relay[2])
                def _(relay=relay):
                    halo_copy(block, piece, relay).wait_recv()
                    halo_pass(block, relay, piece).start()

    def hand_on(block, step):
        pass_far(block, plan.chunks - 1 - step)
        for piece, at in enumerate(plan.steps):
            @pl.when(step == at)
            def _(piece=piece):
                pass_halo(block, piece)

    def at_step(block, step, action, *conditions, **kinds):
        for b in range(BLOCKS):
            if b < block:
                continue
            own = step - (b - block) * plan.chunks
            fits = (own >= 0) & (own < plan.chunks)
            for condition in conditions:
                fits = fits & condition

            @pl.when(fits)
            def _(b=b, own=own):
                action(b, own, **kinds)

    paced = me >= plan.count - plan.plane
    free = me < plan.count - plan.plane
    window = min(WINDOW, plan.chunks - 1)

    @pl.loop(0, plan.chunks + AHEAD)
    def _(step):
        within = (step < window) | free

        @pl.when((step < plan.chunks) & within)
        def _():
            send(0, step)

        if plan.plane:
            @pl.when((step == window) & paced)
            def _():
                send(0, step, direct=False)

            @pl.when((step >= AHEAD) & ((step - AHEAD < window) | free))
            def _():
                hand_on(0, step - AHEAD)

    for load in loads:
        load.wait()

    for block in range(BLOCKS):
        gain[block] = columns(gain_row[block:block + 1, :])
        b_in[block] = columns(b_in_row[block:block + 1, :])
        b_out[block] = columns(b_out_row[block:block + 1, :])
        w_in[block] = w_in_t[block].T

    for block in range(BLOCKS):
        ext, far = exts[block], fars[block]

        @pl.loop(0, plan.chunks)
        def _(step, block=block, ext=ext, far=far):
            number = plan.chunks - 1 - step
            if plan.plane:
                ready = step - LAG + block * plan.chunks

                @pl.when(free & (ready >= 0) & (ready < plan.chunks))
                def _():
                    hand_on(1, ready)

            for index in range(plan.far):
                far_copy(block, index, number).wait_recv()
            for piece, (*_, reader) in enumerate(plan.pieces):
                @pl.when(number == reader)
                def _(piece=piece):
                    halo_copy(block, piece).wait_recv()

            if plan.plane:
                at_step(block, step + window, hand_on, paced)
                at_step(block, step + window, send, paced, relayed=False)
                at_step(block, step + window + 1, send, paced, direct=False)

            col = pl.multiple_of(number * chunk, LANES)
            value = mix_tile(
                rotated_tile(plan, ext, far, col),
                across(gain[block], chunk), w_in[block], across(b_in[block], chunk),
                w_out[block], across(b_out[block], chunk),
            )
            if block + 1 < BLOCKS:
                ext1[:, pl.ds(pl.multiple_of(halo + col, LANES), chunk)] = value[:near]
                sent1[:, pl.ds(col, chunk)] = value[near:]

                @pl.when(free)
                def _():
                    send(1, step)
            else:
                out[:, pl.ds(col, chunk)] = value

    @pl.loop(0, plan.chunks)
    def _(number):
        for block in range(BLOCKS):
            for index in range(plan.far):
                far_copy(block, index, number).wait_send()
            for relay in plan.relays:
                if relay[0] is not None:
                    @pl.when(place == relay[2])
                    def _(relay=relay, block=block):
                        far_pass(block, relay, number).wait_send()

    for block in range(BLOCKS):
        for piece in range(len(plan.pieces)):
            halo_copy(block, piece).wait_send()
            for relay in plan.relays:
                if relay[0] is None:
                    @pl.when(place == relay[2])
                    def _(relay=relay, block=block, piece=piece):
                        halo_pass(block, relay, piece).wait_send()


def plane_of(mesh):
    devices = mesh.devices.reshape(-1)
    if mesh.shape["seq"] != devices.size or not hasattr(devices[0], "coords"):
        return 0
    places = [(*reversed(d.coords), d.core_on_chip) for d in devices]
    shape = tuple(max(p[axis] for p in places) + 1 for axis in range(4))
    plane = shape[1] * shape[2] * shape[3]
    ordered = [(i // plane, i // 4 % 2, i // 2 % 2, i % 2) for i in range(devices.size)]
    return plane if shape[1:] == (2, 2, 2) and shape[0] > 1 and places == ordered else 0


def solution(mesh):
    count = mesh.shape["seq"]
    plane = plane_of(mesh)

    def shards(tokens, norm_gain, in_weight, in_bias, out_weight, out_bias):
        channels, rows = tokens.shape
        plan = Plan(count, rows, min(CHUNK, rows // 2), plane)
        distant = plan.far * TRACK_CH
        wide = plan.halo + rows
        held = [
            pltpu.with_memory_space_constraint(x, pltpu.HBM)
            for x in (tokens, norm_gain, jnp.swapaxes(in_weight, 1, 2), in_bias, out_weight, out_bias)
        ]
        return pl.pallas_call(
            functools.partial(kernel, plan),
            out_shape=pltpu.VMEM(tokens.shape, tokens.dtype),
            in_specs=[pl.BlockSpec(memory_space=pl.ANY)] * len(held),
            out_specs=pl.BlockSpec(memory_space=pltpu.VMEM),
            scratch_shapes=[
                *(pltpu.VMEM(x.shape, x.dtype) for x in held[1:]),
                pltpu.VMEM((BLOCKS, channels, LANES), jnp.float32),
                pltpu.VMEM(in_weight.shape, jnp.bfloat16),
                pltpu.VMEM((BLOCKS, in_weight.shape[1], LANES), jnp.float32),
                pltpu.VMEM((BLOCKS, channels, LANES), jnp.float32),
                pltpu.VMEM((BLOCKS, TRACK_CH, rows), jnp.bfloat16),
                pltpu.VMEM((BLOCKS, plan.near, plan.halo), jnp.bfloat16),
                pltpu.VMEM((plan.near, wide), jnp.bfloat16),
                pltpu.VMEM((plan.near, wide), jnp.bfloat16),
                pltpu.VMEM((distant, rows), jnp.bfloat16),
                pltpu.VMEM((distant, rows), jnp.bfloat16),
                pltpu.VMEM((distant, rows), jnp.bfloat16),
                pltpu.SemaphoreType.DMA((BLOCKS, plan.far, plan.chunks)),
                pltpu.SemaphoreType.DMA((BLOCKS, plan.far, plan.chunks)),
                pltpu.SemaphoreType.DMA((BLOCKS, len(plan.pieces))),
                pltpu.SemaphoreType.DMA((BLOCKS, len(plan.pieces))),
                pltpu.SemaphoreType.DMA((BLOCKS, plan.chunks)),
                pltpu.SemaphoreType.DMA((BLOCKS, plan.chunks)),
                pltpu.SemaphoreType.DMA((BLOCKS, len(plan.pieces))),
                pltpu.SemaphoreType.DMA((BLOCKS, len(plan.pieces))),
                pltpu.SemaphoreType.DMA((len(held),)),
            ],
            compiler_params=pltpu.CompilerParams(
                collective_id=0, has_side_effects=True, vmem_limit_bytes=52 * 2**20
            ),
        )(*held)

    return jax.shard_map(
        shards,
        mesh=mesh,
        in_specs=(P("batch", "seq"), P(), P(), P(), P(), P()),
        out_specs=P("batch", "seq"),
        check_vma=False,
    )
```

```python
import functools

import jax
import jax.numpy as jnp
from jax import lax
from jax.experimental import pallas as pl
from jax.experimental.pallas import tpu as pltpu
from jax.sharding import PartitionSpec as P

TRACK_CH = 16
TRACKS = 19
BLOCKS = 2
LANES = 128
CHUNK = 1024
LAG = 2
AHEAD = 1
WINDOW = 2
MESH = pl.DeviceIdType.MESH


class Plan:
    def __init__(self, count, rows, chunk, plane):
        self.count, self.rows, self.chunk = count, rows, chunk
        self.chunks = rows // chunk
        self.short = 0
        while self.short + 1 < TRACKS and 2**self.short < rows:
            self.short += 1
        self.near = (1 + self.short) * TRACK_CH
        self.distances = [2 ** (t - 1) // rows for t in range(1 + self.short, TRACKS)]
        self.far = len(self.distances)
        self.halo = max(2 ** (self.short - 1), LANES)
        self.pieces = []
        small = sum(1 for t in range(1, 1 + self.short) if 2 ** (t - 1) < LANES)
        self.pieces.append((TRACK_CH, small * TRACK_CH, LANES, LANES, self.chunks - 1, 0))
        for t in range(1 + small, 1 + self.short):
            offset = 2 ** (t - 1)
            width = min(offset, chunk)
            for part in range(offset // width):
                from_end = offset - part * width
                source = (rows - from_end) // chunk
                self.pieces.append((t * TRACK_CH, TRACK_CH, from_end, width, source, part))
        self.pieces.sort(key=lambda piece: (-piece[5], piece[2] if piece[3] < chunk else -piece[2]))
        big = [piece for piece in self.pieces if piece[1] * piece[3] >= TRACK_CH * chunk]
        self.pieces = big + [piece for piece in self.pieces if piece not in big]
        self.steps = [
            max(min(at, self.chunks - 1), self.chunks - 1 - piece[4]) for at, piece in enumerate(self.pieces)
        ]
        self.plane = plane
        self.relays = []
        if plane:
            last = plane - 1
            self.relays = [(0, last, 2, 0), (None, last, 3, 0), (1, last - 1, 0, 0), (1, last, 1, 1)]
        peers = []
        hops = [1] + self.distances
        for _, sender, relay, receiver in self.relays:
            hops += [(relay - sender) % count, (plane + receiver - relay) % count]
        for d in hops:
            for signed in (d, count - d):
                if signed % count and signed % count not in peers:
                    peers.append(signed % count)
        self.peers = peers


def rotated_tile(plan, ext, far, col):
    tile, halo = plan.chunk, plan.halo
    parts = []
    for t in range(1 + plan.short):
        rows = pl.ds(t * TRACK_CH, TRACK_CH)
        offset = 0 if t == 0 else 2 ** (t - 1)
        if offset % LANES == 0:
            start = pl.multiple_of(halo - offset + col, LANES)
            parts.append(ext[rows, pl.ds(start, tile)].astype(jnp.float32))
        else:
            start = pl.multiple_of(halo - LANES + col, LANES)
            window = ext[rows, pl.ds(start, tile + LANES)].astype(jnp.float32)
            parts.append(pltpu.roll(window, offset, 1)[:, LANES:])
    parts.append(far[:, pl.ds(pl.multiple_of(col, LANES), tile)].astype(jnp.float32))
    return jnp.concatenate(parts, 0)


def columns(row):
    return jnp.broadcast_to(row, (LANES, row.shape[1])).T


def across(column, width):
    return jnp.concatenate([column] * (width // LANES), 1)


def mix_tile(as_float, gain, in_weight, in_bias, out_weight, out_bias):
    mean_square = jnp.mean(as_float * as_float, axis=0, keepdims=True)
    normed = (as_float * gain * lax.rsqrt(mean_square + 1e-06)).astype(jnp.bfloat16)
    pre_act = jnp.dot(in_weight, normed, preferred_element_type=jnp.float32) + in_bias
    inner = pre_act * (0.7978845608028654 + 0.035677408136300125 * (pre_act * pre_act))
    half = 0.5 * pre_act
    active = (half + half * jnp.tanh(inner)).astype(jnp.bfloat16)
    summed = as_float + jnp.dot(out_weight, active, preferred_element_type=jnp.float32) + out_bias
    return summed.astype(jnp.bfloat16)


def kernel(plan, tokens, gain_in, w_in_in, b_in_in, w_out_in, b_out_in, out,
           gain_row, w_in_t, b_in_row, w_out, b_out_row, gain, w_in, b_in, b_out,
           relay_far, relay_halo, ext0, ext1, far0, far1, sent1,
           far_send, far_recv, halo_send, halo_recv,
           pass_send, pass_recv, pass_halo_send, pass_halo_recv, load_sem):
    me = lax.axis_index("seq")
    chunk, near, halo, rows = plan.chunk, plan.near, plan.halo, plan.rows
    exts, fars = (ext0, ext1), (far0, far1)

    loads = [
        pltpu.make_async_copy(source, target, load_sem.at[at])
        for at, (source, target) in enumerate((
            (gain_in, gain_row), (w_in_in, w_in_t), (b_in_in, b_in_row), (w_out_in, w_out), (b_out_in, b_out_row),
            (tokens.at[pl.ds(0, near), :], ext0.at[:, pl.ds(halo, rows)]),
        ))
    ]
    for load in loads:
        load.start()

    barrier = pltpu.get_barrier_semaphore()
    for peer in plan.peers:
        pl.semaphore_signal(barrier, inc=1, device_id={"seq": lax.rem(me + peer, plan.count)}, device_id_type=MESH)
    pl.semaphore_wait(barrier, len(plan.peers))

    place = lax.rem(me, plan.plane) if plan.plane else me

    def along(hop):
        return {"seq": lax.rem(me + hop + plan.count, plan.count)}

    def far_copy(block, index, number, relay=None):
        cols = pl.ds(pl.multiple_of(number * chunk, LANES), chunk)
        if block == 0:
            source = tokens.at[pl.ds(near + index * TRACK_CH, TRACK_CH), cols]
        else:
            source = sent1.at[pl.ds(index * TRACK_CH, TRACK_CH), cols]
        if relay is None:
            target = fars[block].at[pl.ds(index * TRACK_CH, TRACK_CH), cols]
            arrived, hop = far_recv.at[block, index, number], plan.distances[index]
        else:
            target, arrived, hop = relay_far.at[block, :, cols], pass_recv.at[block, number], relay[2] - relay[1]
        return pltpu.make_async_remote_copy(
            src_ref=source, dst_ref=target, send_sem=far_send.at[block, index, number], recv_sem=arrived,
            device_id=along(hop), device_id_type=MESH,
        )

    def far_pass(block, relay, number):
        index, _, at, receiver = relay
        cols = pl.ds(pl.multiple_of(number * chunk, LANES), chunk)
        return pltpu.make_async_remote_copy(
            src_ref=relay_far.at[block, :, cols],
            dst_ref=fars[block].at[pl.ds(index * TRACK_CH, TRACK_CH), cols],
            send_sem=pass_send.at[block, number],
            recv_sem=far_recv.at[block, index, number],
            device_id=along(plan.plane + receiver - at), device_id_type=MESH,
        )

    def halo_copy(block, number, relay=None):
        first, height, from_end, width, _, _ = plan.pieces[number]
        where = (pl.ds(first, height), pl.ds(halo - from_end, width))
        if block == 0:
            source = tokens.at[pl.ds(first, height), pl.ds(rows - from_end, width)]
        else:
            source = ext1.at[pl.ds(first, height), pl.ds(halo + rows - from_end, width)]
        if relay is None:
            target, arrived, hop = exts[block].at[where], halo_recv.at[block, number], 1
        else:
            target, arrived = relay_halo.at[(block, *where)], pass_halo_recv.at[block, number]
            hop = relay[2] - relay[1]
        return pltpu.make_async_remote_copy(
            src_ref=source, dst_ref=target, send_sem=halo_send.at[block, number], recv_sem=arrived,
            device_id=along(hop), device_id_type=MESH,
        )

    def halo_pass(block, relay, number):
        first, height, from_end, width, _, _ = plan.pieces[number]
        where = (pl.ds(first, height), pl.ds(halo - from_end, width))
        return pltpu.make_async_remote_copy(
            src_ref=relay_halo.at[(block, *where)],
            dst_ref=exts[block].at[where],
            send_sem=pass_halo_send.at[block, number],
            recv_sem=halo_recv.at[block, number],
            device_id=along(plan.plane + relay[3] - relay[2]), device_id_type=MESH,
        )

    def start(make, key, *args, direct=True, relayed=True):
        relays = [relay for relay in plan.relays if relay[0] == key]
        if relayed:
            for relay in relays:
                @pl.when(place == relay[1])
                def _(relay=relay):
                    make(*args, relay=relay).start()

        if direct and relays:
            own = place >= 0
            for relay in relays:
                own = own & (place != relay[1])

            @pl.when(own)
            def _():
                make(*args).start()
        elif direct:
            make(*args).start()

    def send(block, step, **kinds):
        for index in reversed(range(plan.far)):
            start(far_copy, index, block, index, plan.chunks - 1 - step, **kinds)
        for piece, at in enumerate(plan.steps):
            @pl.when(step == at)
            def _(piece=piece):
                start(halo_copy, None, block, piece, **kinds)

    def pass_far(block, number):
        for relay in plan.relays:
            if relay[0] is not None:
                @pl.when(place == relay[2])
                def _(relay=relay):
                    far_copy(block, relay[0], number, relay).wait_recv()
                    far_pass(block, relay, number).start()

    def pass_halo(block, piece):
        for relay in plan.relays:
            if relay[0] is None:
                @pl.when(place == relay[2])
                def _(relay=relay):
                    halo_copy(block, piece, relay).wait_recv()
                    halo_pass(block, relay, piece).start()

    def hand_on(block, step):
        pass_far(block, plan.chunks - 1 - step)
        for piece, at in enumerate(plan.steps):
            @pl.when(step == at)
            def _(piece=piece):
                pass_halo(block, piece)

    def at_step(block, step, action, *conditions, **kinds):
        for b in range(BLOCKS):
            if b < block:
                continue
            own = step - (b - block) * plan.chunks
            fits = (own >= 0) & (own < plan.chunks)
            for condition in conditions:
                fits = fits & condition

            @pl.when(fits)
            def _(b=b, own=own):
                action(b, own, **kinds)

    paced = me >= plan.count - plan.plane
    free = me < plan.count - plan.plane
    window = min(WINDOW, plan.chunks - 1)

    @pl.loop(0, plan.chunks + AHEAD)
    def _(step):
        within = (step < window) | free

        @pl.when((step < plan.chunks) & within)
        def _():
            send(0, step)

        if plan.plane:
            @pl.when((step == window) & paced)
            def _():
                send(0, step, direct=False)

            @pl.when((step >= AHEAD) & ((step - AHEAD < window) | free))
            def _():
                hand_on(0, step - AHEAD)

    for load in loads:
        load.wait()

    for block in range(BLOCKS):
        gain[block] = columns(gain_row[block:block + 1, :])
        b_in[block] = columns(b_in_row[block:block + 1, :])
        b_out[block] = columns(b_out_row[block:block + 1, :])
        w_in[block] = w_in_t[block].T

    for block in range(BLOCKS):
        ext, far = exts[block], fars[block]

        @pl.loop(0, plan.chunks)
        def _(step, block=block, ext=ext, far=far):
            number = plan.chunks - 1 - step
            if plan.plane:
                ready = step - LAG + block * plan.chunks

                @pl.when(free & (ready >= 0) & (ready < plan.chunks))
                def _():
                    hand_on(1, ready)

            for index in range(plan.far):
                far_copy(block, index, number).wait_recv()
            for piece, (*_, reader) in enumerate(plan.pieces):
                @pl.when(number == reader)
                def _(piece=piece):
                    halo_copy(block, piece).wait_recv()

            if plan.plane:
                at_step(block, step + window, hand_on, paced)
                at_step(block, step + window, send, paced, relayed=False)
                at_step(block, step + window + 1, send, paced, direct=False)

            col = pl.multiple_of(number * chunk, LANES)
            value = mix_tile(
                rotated_tile(plan, ext, far, col),
                across(gain[block], chunk), w_in[block], across(b_in[block], chunk),
                w_out[block], across(b_out[block], chunk),
            )
            if block + 1 < BLOCKS:
                ext1[:, pl.ds(pl.multiple_of(halo + col, LANES), chunk)] = value[:near]
                sent1[:, pl.ds(col, chunk)] = value[near:]

                @pl.when(free)
                def _():
                    send(1, step)
            else:
                out[:, pl.ds(col, chunk)] = value

    @pl.loop(0, plan.chunks)
    def _(number):
        for block in range(BLOCKS):
            for index in range(plan.far):
                far_copy(block, index, number).wait_send()
            for relay in plan.relays:
                if relay[0] is not None:
                    @pl.when(place == relay[2])
                    def _(relay=relay, block=block):
                        far_pass(block, relay, number).wait_send()

    for block in range(BLOCKS):
        for piece in range(len(plan.pieces)):
            halo_copy(block, piece).wait_send()
            for relay in plan.relays:
                if relay[0] is None:
                    @pl.when(place == relay[2])
                    def _(relay=relay, block=block, piece=piece):
                        halo_pass(block, relay, piece).wait_send()


def plane_of(mesh):
    devices = mesh.devices.reshape(-1)
    if mesh.shape["seq"] != devices.size or not hasattr(devices[0], "coords"):
        return 0
    places = [(*reversed(d.coords), d.core_on_chip) for d in devices]
    shape = tuple(max(p[axis] for p in places) + 1 for axis in range(4))
    plane = shape[1] * shape[2] * shape[3]
    ordered = [(i // plane, i // 4 % 2, i // 2 % 2, i % 2) for i in range(devices.size)]
    return plane if shape[1:] == (2, 2, 2) and shape[0] > 1 and places == ordered else 0


def solution(mesh):
    count = mesh.shape["seq"]
    plane = plane_of(mesh)

    def shards(tokens, norm_gain, in_weight, in_bias, out_weight, out_bias):
        channels, rows = tokens.shape
        plan = Plan(count, rows, min(CHUNK, rows // 2), plane)
        distant = plan.far * TRACK_CH
        wide = plan.halo + rows
        held = [
            pltpu.with_memory_space_constraint(x, pltpu.HBM)
            for x in (tokens, norm_gain, jnp.swapaxes(in_weight, 1, 2), in_bias, out_weight, out_bias)
        ]
        return pl.pallas_call(
            functools.partial(kernel, plan),
            out_shape=pltpu.VMEM(tokens.shape, tokens.dtype),
            in_specs=[pl.BlockSpec(memory_space=pl.ANY)] * len(held),
            out_specs=pl.BlockSpec(memory_space=pltpu.VMEM),
            scratch_shapes=[
                *(pltpu.VMEM(x.shape, x.dtype) for x in held[1:]),
                pltpu.VMEM((BLOCKS, channels, LANES), jnp.float32),
                pltpu.VMEM(in_weight.shape, jnp.bfloat16),
                pltpu.VMEM((BLOCKS, in_weight.shape[1], LANES), jnp.float32),
                pltpu.VMEM((BLOCKS, channels, LANES), jnp.float32),
                pltpu.VMEM((BLOCKS, TRACK_CH, rows), jnp.bfloat16),
                pltpu.VMEM((BLOCKS, plan.near, plan.halo), jnp.bfloat16),
                pltpu.VMEM((plan.near, wide), jnp.bfloat16),
                pltpu.VMEM((plan.near, wide), jnp.bfloat16),
                pltpu.VMEM((distant, rows), jnp.bfloat16),
                pltpu.VMEM((distant, rows), jnp.bfloat16),
                pltpu.VMEM((distant, rows), jnp.bfloat16),
                pltpu.SemaphoreType.DMA((BLOCKS, plan.far, plan.chunks)),
                pltpu.SemaphoreType.DMA((BLOCKS, plan.far, plan.chunks)),
                pltpu.SemaphoreType.DMA((BLOCKS, len(plan.pieces))),
                pltpu.SemaphoreType.DMA((BLOCKS, len(plan.pieces))),
                pltpu.SemaphoreType.DMA((BLOCKS, plan.chunks)),
                pltpu.SemaphoreType.DMA((BLOCKS, plan.chunks)),
                pltpu.SemaphoreType.DMA((BLOCKS, len(plan.pieces))),
                pltpu.SemaphoreType.DMA((BLOCKS, len(plan.pieces))),
                pltpu.SemaphoreType.DMA((len(held),)),
            ],
            compiler_params=pltpu.CompilerParams(
                collective_id=0, has_side_effects=True, vmem_limit_bytes=52 * 2**20
            ),
        )(*held)

    return jax.shard_map(
        shards,
        mesh=mesh,
        in_specs=(P("batch", "seq"), P(), P(), P(), P(), P()),
        out_specs=P("batch", "seq"),
        check_vma=False,
    )
```

```python
import functools

import jax
import jax.numpy as jnp
from jax import lax
from jax.experimental import pallas as pl
from jax.experimental.pallas import tpu as pltpu
from jax.sharding import PartitionSpec as P

TRACK_CH = 16
TRACKS = 19
BLOCKS = 2
LANES = 128
CHUNK = 1024
LAG = 2
AHEAD = 1
STAGES = ((0, 2),)
MESH = pl.DeviceIdType.MESH


class Plan:
    def __init__(self, count, rows, chunk, plane):
        self.count, self.rows, self.chunk = count, rows, chunk
        self.chunks = rows // chunk
        self.short = 0
        while self.short + 1 < TRACKS and 2**self.short < rows:
            self.short += 1
        self.near = (1 + self.short) * TRACK_CH
        self.distances = [2 ** (t - 1) // rows for t in range(1 + self.short, TRACKS)]
        self.far = len(self.distances)
        self.halo = max(2 ** (self.short - 1), LANES)
        self.pieces = []
        small = sum(1 for t in range(1, 1 + self.short) if 2 ** (t - 1) < LANES)
        self.pieces.append((TRACK_CH, small * TRACK_CH, LANES, LANES, self.chunks - 1, 0))
        for t in range(1 + small, 1 + self.short):
            offset = 2 ** (t - 1)
            width = min(offset, chunk)
            for part in range(offset // width):
                from_end = offset - part * width
                source = (rows - from_end) // chunk
                self.pieces.append((t * TRACK_CH, TRACK_CH, from_end, width, source, part))
        self.pieces.sort(key=lambda piece: (piece[1] * piece[3] >= TRACK_CH * chunk, -piece[0], -piece[5], piece[2]))
        held, self.steps = 0, []
        for piece in self.pieces:
            self.steps.append(max(held // (TRACK_CH * chunk), self.chunks - 1 - piece[4]))
            held += piece[1] * piece[3]
        ends = [first for first, _ in STAGES[1:]] + [BLOCKS * self.chunks]
        self.stages = [(first, min(end, BLOCKS * self.chunks), width) for (first, width), end in zip(STAGES, ends)]
        self.plane = plane
        self.relays = []
        if plane:
            last = plane - 1
            self.relays = [(0, last, 2, 0), (None, last, 3, 0), (1, last - 1, 0, 0), (1, last, 1, 1)]
        peers = []
        hops = [1] + self.distances
        for _, sender, relay, receiver in self.relays:
            hops += [(relay - sender) % count, (plane + receiver - relay) % count]
        for d in hops:
            for signed in (d, count - d):
                if signed % count and signed % count not in peers:
                    peers.append(signed % count)
        self.peers = peers


def rotated_tile(plan, ext, far, col):
    tile, halo = plan.chunk, plan.halo
    parts = []
    for t in range(1 + plan.short):
        rows = pl.ds(t * TRACK_CH, TRACK_CH)
        offset = 0 if t == 0 else 2 ** (t - 1)
        if offset % LANES == 0:
            start = pl.multiple_of(halo - offset + col, LANES)
            parts.append(ext[rows, pl.ds(start, tile)].astype(jnp.float32))
        else:
            start = pl.multiple_of(halo - LANES + col, LANES)
            window = ext[rows, pl.ds(start, tile + LANES)].astype(jnp.float32)
            parts.append(pltpu.roll(window, offset, 1)[:, LANES:])
    parts.append(far[:, pl.ds(pl.multiple_of(col, LANES), tile)].astype(jnp.float32))
    return jnp.concatenate(parts, 0)


def columns(row):
    return jnp.broadcast_to(row, (LANES, row.shape[1])).T


def across(column, width):
    return jnp.concatenate([column] * (width // LANES), 1)


def mix_tile(as_float, gain, in_weight, in_bias, out_weight, out_bias):
    mean_square = jnp.mean(as_float * as_float, axis=0, keepdims=True)
    normed = (as_float * gain * lax.rsqrt(mean_square + 1e-06)).astype(jnp.bfloat16)
    pre_act = jnp.dot(in_weight, normed, preferred_element_type=jnp.float32) + in_bias
    inner = pre_act * (0.7978845608028654 + 0.035677408136300125 * (pre_act * pre_act))
    half = 0.5 * pre_act
    active = (half + half * jnp.tanh(inner)).astype(jnp.bfloat16)
    summed = as_float + jnp.dot(out_weight, active, preferred_element_type=jnp.float32) + out_bias
    return summed.astype(jnp.bfloat16)


def kernel(plan, tokens, gain_in, w_in_in, b_in_in, w_out_in, b_out_in, out, last, gain, w_in, b_in, w_out, b_out,
           gain_row, w_in_t, b_in_row, b_out_row,
           relay_far, relay_halo, ext0, ext1, far0, far1, sent1,
           far_send, far_recv, halo_send, halo_recv,
           pass_send, pass_recv, pass_halo_send, pass_halo_recv, load_sem):
    me = lax.axis_index("seq")
    chunk, near, halo, rows = plan.chunk, plan.near, plan.halo, plan.rows
    exts, fars = (ext0, ext1), (far0, far1)

    loads = [
        pltpu.make_async_copy(source, target, load_sem.at[at])
        for at, (source, target) in enumerate((
            (gain_in, gain_row), (w_in_in, w_in_t), (b_in_in, b_in_row), (w_out_in, w_out), (b_out_in, b_out_row),
            (tokens.at[pl.ds(0, near), :], ext0.at[:, pl.ds(halo, rows)]),
        ))
    ]
    for load in loads:
        load.start()

    barrier = pltpu.get_barrier_semaphore()
    for peer in plan.peers:
        pl.semaphore_signal(barrier, inc=1, device_id={"seq": lax.rem(me + peer, plan.count)}, device_id_type=MESH)
    pl.semaphore_wait(barrier, len(plan.peers))

    place = lax.rem(me, plan.plane) if plan.plane else me

    def along(hop):
        return {"seq": lax.rem(me + hop + plan.count, plan.count)}

    def far_copy(block, index, number, relay=None):
        cols = pl.ds(pl.multiple_of(number * chunk, LANES), chunk)
        if block == 0:
            source = tokens.at[pl.ds(near + index * TRACK_CH, TRACK_CH), cols]
        else:
            source = sent1.at[pl.ds(index * TRACK_CH, TRACK_CH), cols]
        if relay is None:
            target = fars[block].at[pl.ds(index * TRACK_CH, TRACK_CH), cols]
            arrived, hop = far_recv.at[block, index, number], plan.distances[index]
        else:
            target, arrived, hop = relay_far.at[block, :, cols], pass_recv.at[block, number], relay[2] - relay[1]
        return pltpu.make_async_remote_copy(
            src_ref=source, dst_ref=target, send_sem=far_send.at[block, index, number], recv_sem=arrived,
            device_id=along(hop), device_id_type=MESH,
        )

    def far_pass(block, relay, number):
        index, _, at, receiver = relay
        cols = pl.ds(pl.multiple_of(number * chunk, LANES), chunk)
        return pltpu.make_async_remote_copy(
            src_ref=relay_far.at[block, :, cols],
            dst_ref=fars[block].at[pl.ds(index * TRACK_CH, TRACK_CH), cols],
            send_sem=pass_send.at[block, number],
            recv_sem=far_recv.at[block, index, number],
            device_id=along(plan.plane + receiver - at), device_id_type=MESH,
        )

    def halo_copy(block, number, relay=None):
        first, height, from_end, width, _, _ = plan.pieces[number]
        where = (pl.ds(first, height), pl.ds(halo - from_end, width))
        if block == 0:
            source = tokens.at[pl.ds(first, height), pl.ds(rows - from_end, width)]
        else:
            source = ext1.at[pl.ds(first, height), pl.ds(halo + rows - from_end, width)]
        if relay is None:
            target, arrived, hop = exts[block].at[where], halo_recv.at[block, number], 1
        else:
            target, arrived = relay_halo.at[(block, *where)], pass_halo_recv.at[block, number]
            hop = relay[2] - relay[1]
        return pltpu.make_async_remote_copy(
            src_ref=source, dst_ref=target, send_sem=halo_send.at[block, number], recv_sem=arrived,
            device_id=along(hop), device_id_type=MESH,
        )

    def halo_pass(block, relay, number):
        first, height, from_end, width, _, _ = plan.pieces[number]
        where = (pl.ds(first, height), pl.ds(halo - from_end, width))
        return pltpu.make_async_remote_copy(
            src_ref=relay_halo.at[(block, *where)],
            dst_ref=exts[block].at[where],
            send_sem=pass_halo_send.at[block, number],
            recv_sem=halo_recv.at[block, number],
            device_id=along(plan.plane + relay[3] - relay[2]), device_id_type=MESH,
        )

    def start(make, key, *args, direct=True, relayed=True):
        relays = [relay for relay in plan.relays if relay[0] == key]
        if relayed:
            for relay in relays:
                @pl.when(place == relay[1])
                def _(relay=relay):
                    make(*args, relay=relay).start()

        if direct and relays:
            own = place >= 0
            for relay in relays:
                own = own & (place != relay[1])

            @pl.when(own)
            def _():
                make(*args).start()
        elif direct:
            make(*args).start()

    def send(block, step, **kinds):
        for index in reversed(range(plan.far)):
            start(far_copy, index, block, index, plan.chunks - 1 - step, **kinds)
        for piece, at in enumerate(plan.steps):
            @pl.when(step == at)
            def _(piece=piece):
                start(halo_copy, None, block, piece, **kinds)

    def pass_far(block, number):
        for relay in plan.relays:
            if relay[0] is not None:
                @pl.when(place == relay[2])
                def _(relay=relay):
                    far_copy(block, relay[0], number, relay).wait_recv()
                    far_pass(block, relay, number).start()

    def pass_halo(block, piece):
        for relay in plan.relays:
            if relay[0] is None:
                @pl.when(place == relay[2])
                def _(relay=relay):
                    halo_copy(block, piece, relay).wait_recv()
                    halo_pass(block, relay, piece).start()

    def hand_on(block, step):
        pass_far(block, plan.chunks - 1 - step)
        for piece, at in enumerate(plan.steps):
            @pl.when(step == at)
            def _(piece=piece):
                pass_halo(block, piece)

    def at_stage(block, step, lead, action, **kinds):
        for first, end, width in plan.stages:
            at = block * plan.chunks + step + width + lead
            for b in range(block, BLOCKS):
                low, high = max(first, b * plan.chunks), min(end, (b + 1) * plan.chunks)
                if low < high:
                    @pl.when(paced & (at >= low) & (at < high))
                    def _(b=b, at=at):
                        action(b, at - b * plan.chunks, **kinds)

    paced = me >= plan.count - plan.plane
    free = me < plan.count - plan.plane

    @pl.loop(0, plan.chunks + AHEAD)
    def _(step):
        @pl.when((step < plan.chunks) & free)
        def _():
            send(0, step)

        if plan.plane:
            width = plan.stages[0][2]

            @pl.when((step < width) & paced)
            def _():
                send(0, step, relayed=False)

            @pl.when((step < width + 1) & paced)
            def _():
                send(0, step, direct=False)

            @pl.when((step >= AHEAD) & (step - AHEAD < plan.chunks) & ((step - AHEAD < width) | free))
            def _():
                hand_on(0, step - AHEAD)

    for load in loads:
        load.wait()

    for block in range(BLOCKS):
        gain[block] = columns(gain_row[block:block + 1, :])
        b_in[block] = columns(b_in_row[block:block + 1, :])
        b_out[block] = columns(b_out_row[block:block + 1, :])
        w_in[block] = w_in_t[block].T

    for block in range(BLOCKS):
        ext, far = exts[block], fars[block]

        def advance(step, block=block, ext=ext, far=far, final=False):
            number = plan.chunks - 1 - step
            if plan.plane:
                ready = step - LAG + block * plan.chunks

                @pl.when(free & (ready >= 0) & (ready < plan.chunks))
                def _():
                    hand_on(1, ready)

            for index in range(plan.far):
                far_copy(block, index, number).wait_recv()
            for piece, (*_, reader) in enumerate(plan.pieces):
                @pl.when(number == reader)
                def _(piece=piece):
                    halo_copy(block, piece).wait_recv()

            if plan.plane:
                at_stage(block, step, 0, hand_on)
                at_stage(block, step, 0, send, relayed=False)
                at_stage(block, step, 1, send, direct=False)

            if final:
                last[...] = rotated_tile(plan, ext, far, 0).astype(jnp.bfloat16)
                return

            col = pl.multiple_of(number * chunk, LANES)
            value = mix_tile(
                rotated_tile(plan, ext, far, col),
                across(gain[block], chunk), w_in[block], across(b_in[block], chunk),
                w_out[block], across(b_out[block], chunk),
            )
            if block + 1 < BLOCKS:
                ext1[:, pl.ds(pl.multiple_of(halo + col, LANES), chunk)] = value[:near]
                sent1[:, pl.ds(col, chunk)] = value[near:]

                @pl.when(free)
                def _():
                    send(1, step)
            else:
                out[:, pl.ds(col, chunk)] = value

        if block + 1 < BLOCKS:
            pl.loop(0, plan.chunks)(advance)
        else:
            pl.loop(0, plan.chunks - 1)(advance)
            advance(plan.chunks - 1, final=True)

    @pl.loop(0, plan.chunks)
    def _(number):
        for block in range(BLOCKS):
            for index in range(plan.far):
                far_copy(block, index, number).wait_send()
            for relay in plan.relays:
                if relay[0] is not None:
                    @pl.when(place == relay[2])
                    def _(relay=relay, block=block):
                        far_pass(block, relay, number).wait_send()

    for block in range(BLOCKS):
        for piece in range(len(plan.pieces)):
            halo_copy(block, piece).wait_send()
            for relay in plan.relays:
                if relay[0] is None:
                    @pl.when(place == relay[2])
                    def _(relay=relay, block=block, piece=piece):
                        halo_pass(block, relay, piece).wait_send()


def finish(chunk, done, last, gain, w_in, b_in, w_out, b_out, out, tail, sems):
    rest = pl.ds(chunk, done.shape[1] - chunk)
    body = pltpu.make_async_copy(done.at[:, rest], out.at[:, rest], sems.at[0])
    body.start()
    block = BLOCKS - 1
    tail[...] = mix_tile(
        last[...].astype(jnp.float32),
        across(gain[block], chunk), w_in[block], across(b_in[block], chunk),
        w_out[block], across(b_out[block], chunk),
    )
    end = pltpu.make_async_copy(tail, out.at[:, pl.ds(0, chunk)], sems.at[1])
    end.start()
    body.wait()
    end.wait()


def plane_of(mesh):
    devices = mesh.devices.reshape(-1)
    if mesh.shape["seq"] != devices.size or not hasattr(devices[0], "coords"):
        return 0
    places = [(*reversed(d.coords), d.core_on_chip) for d in devices]
    shape = tuple(max(p[axis] for p in places) + 1 for axis in range(4))
    plane = shape[1] * shape[2] * shape[3]
    ordered = [(i // plane, i // 4 % 2, i // 2 % 2, i % 2) for i in range(devices.size)]
    return plane if shape[1:] == (2, 2, 2) and shape[0] > 1 and places == ordered else 0


def solution(mesh):
    count = mesh.shape["seq"]
    plane = plane_of(mesh)

    def shards(tokens, norm_gain, in_weight, in_bias, out_weight, out_bias):
        channels, rows = tokens.shape
        plan = Plan(count, rows, min(CHUNK, rows // 2), plane)
        distant = plan.far * TRACK_CH
        wide = plan.halo + rows
        held = [
            pltpu.with_memory_space_constraint(x, pltpu.HBM)
            for x in (tokens, norm_gain, jnp.swapaxes(in_weight, 1, 2), in_bias, out_weight, out_bias)
        ]
        kept = pl.pallas_call(
            functools.partial(kernel, plan),
            out_shape=[
                pltpu.VMEM(tokens.shape, tokens.dtype),
                pltpu.VMEM((channels, plan.chunk), tokens.dtype),
                pltpu.VMEM((BLOCKS, channels, LANES), jnp.float32),
                pltpu.VMEM(in_weight.shape, jnp.bfloat16),
                pltpu.VMEM((BLOCKS, in_weight.shape[1], LANES), jnp.float32),
                pltpu.VMEM(out_weight.shape, jnp.bfloat16),
                pltpu.VMEM((BLOCKS, channels, LANES), jnp.float32),
            ],
            in_specs=[pl.BlockSpec(memory_space=pl.ANY)] * len(held),
            out_specs=[pl.BlockSpec(memory_space=pltpu.VMEM)] * 7,
            scratch_shapes=[
                *(pltpu.VMEM(held[at].shape, held[at].dtype) for at in (1, 2, 3, 5)),
                pltpu.VMEM((BLOCKS, TRACK_CH, rows), jnp.bfloat16),
                pltpu.VMEM((BLOCKS, plan.near, plan.halo), jnp.bfloat16),
                pltpu.VMEM((plan.near, wide), jnp.bfloat16),
                pltpu.VMEM((plan.near, wide), jnp.bfloat16),
                pltpu.VMEM((distant, rows), jnp.bfloat16),
                pltpu.VMEM((distant, rows), jnp.bfloat16),
                pltpu.VMEM((distant, rows), jnp.bfloat16),
                pltpu.SemaphoreType.DMA((BLOCKS, plan.far, plan.chunks)),
                pltpu.SemaphoreType.DMA((BLOCKS, plan.far, plan.chunks)),
                pltpu.SemaphoreType.DMA((BLOCKS, len(plan.pieces))),
                pltpu.SemaphoreType.DMA((BLOCKS, len(plan.pieces))),
                pltpu.SemaphoreType.DMA((BLOCKS, plan.chunks)),
                pltpu.SemaphoreType.DMA((BLOCKS, plan.chunks)),
                pltpu.SemaphoreType.DMA((BLOCKS, len(plan.pieces))),
                pltpu.SemaphoreType.DMA((BLOCKS, len(plan.pieces))),
                pltpu.SemaphoreType.DMA((len(held),)),
            ],
            compiler_params=pltpu.CompilerParams(
                collective_id=0, has_side_effects=True, vmem_limit_bytes=46 * 2**20
            ),
        )(*held)
        return pl.pallas_call(
            functools.partial(finish, plan.chunk),
            out_shape=jax.ShapeDtypeStruct(tokens.shape, tokens.dtype),
            in_specs=[pl.BlockSpec(memory_space=pltpu.VMEM)] * len(kept),
            out_specs=pl.BlockSpec(memory_space=pl.ANY),
            scratch_shapes=[
                pltpu.VMEM((channels, plan.chunk), tokens.dtype),
                pltpu.SemaphoreType.DMA((2,)),
            ],
            compiler_params=pltpu.CompilerParams(vmem_limit_bytes=14 * 2**20),
        )(*kept)

    return jax.shard_map(
        shards,
        mesh=mesh,
        in_specs=(P("batch", "seq"), P(), P(), P(), P(), P()),
        out_specs=P("batch", "seq"),
        check_vma=False,
    )
```

```python
import functools

import jax
import jax.numpy as jnp
from jax import lax
from jax.experimental import pallas as pl
from jax.experimental.pallas import tpu as pltpu
from jax.sharding import PartitionSpec as P

TRACK_CH = 16
TRACKS = 19
BLOCKS = 2
LANES = 128
CHUNK = 1024
LAG = 2
AHEAD = 1
HELD = 4
STAGES = ((0, 2),)
MESH = pl.DeviceIdType.MESH


class Plan:
    def __init__(self, count, rows, chunk, plane):
        self.count, self.rows, self.chunk = count, rows, chunk
        self.chunks = rows // chunk
        self.short = 0
        while self.short + 1 < TRACKS and 2**self.short < rows:
            self.short += 1
        self.near = (1 + self.short) * TRACK_CH
        self.distances = [2 ** (t - 1) // rows for t in range(1 + self.short, TRACKS)]
        self.far = len(self.distances)
        self.halo = max(2 ** (self.short - 1), LANES)
        self.pieces = []
        small = sum(1 for t in range(1, 1 + self.short) if 2 ** (t - 1) < LANES)
        self.pieces.append((TRACK_CH, small * TRACK_CH, LANES, LANES, self.chunks - 1, 0))
        for t in range(1 + small, 1 + self.short):
            offset = 2 ** (t - 1)
            width = min(offset, chunk)
            for part in range(offset // width):
                from_end = offset - part * width
                source = (rows - from_end) // chunk
                self.pieces.append((t * TRACK_CH, TRACK_CH, from_end, width, source, part))
        self.pieces.sort(key=lambda piece: (piece[1] * piece[3] >= TRACK_CH * chunk, -piece[0], -piece[5], piece[2]))
        held, self.steps = 0, []
        for piece in self.pieces:
            self.steps.append(max(held // (TRACK_CH * chunk), self.chunks - 1 - piece[4]))
            held += piece[1] * piece[3]
        ends = [first for first, _ in STAGES[1:]] + [BLOCKS * self.chunks]
        self.stages = [(first, min(end, BLOCKS * self.chunks), width) for (first, width), end in zip(STAGES, ends)]
        self.plane = plane
        self.relays = []
        if plane:
            last = plane - 1
            self.relays = [(0, last, 2, 0), (None, last, 3, 0), (1, last - 1, 0, 0), (1, last, 1, 1)]
        peers = []
        hops = [1] + self.distances
        for _, sender, relay, receiver in self.relays:
            hops += [(relay - sender) % count, (plane + receiver - relay) % count]
        for d in hops:
            for signed in (d, count - d):
                if signed % count and signed % count not in peers:
                    peers.append(signed % count)
        self.peers = peers


def rotated_tile(plan, ext, far, col):
    tile, halo = plan.chunk, plan.halo
    parts = []
    for t in range(1 + plan.short):
        rows = pl.ds(t * TRACK_CH, TRACK_CH)
        offset = 0 if t == 0 else 2 ** (t - 1)
        if offset % LANES == 0:
            start = pl.multiple_of(halo - offset + col, LANES)
            parts.append(ext[rows, pl.ds(start, tile)].astype(jnp.float32))
        else:
            start = pl.multiple_of(halo - LANES + col, LANES)
            window = ext[rows, pl.ds(start, tile + LANES)].astype(jnp.float32)
            parts.append(pltpu.roll(window, offset, 1)[:, LANES:])
    parts.append(far[:, pl.ds(pl.multiple_of(col, LANES), tile)].astype(jnp.float32))
    return jnp.concatenate(parts, 0)


def columns(row):
    return jnp.broadcast_to(row, (LANES, row.shape[1])).T


def across(column, width):
    return jnp.concatenate([column] * (width // LANES), 1)


def mix_tile(as_float, gain, in_weight, in_bias, out_weight, out_bias):
    mean_square = jnp.mean(as_float * as_float, axis=0, keepdims=True)
    normed = (as_float * gain * lax.rsqrt(mean_square + 1e-06)).astype(jnp.bfloat16)
    pre_act = jnp.dot(in_weight, normed, preferred_element_type=jnp.float32) + in_bias
    inner = pre_act * (0.7978845608028654 + 0.035677408136300125 * (pre_act * pre_act))
    half = 0.5 * pre_act
    active = (half + half * jnp.tanh(inner)).astype(jnp.bfloat16)
    summed = as_float + jnp.dot(out_weight, active, preferred_element_type=jnp.float32) + out_bias
    return summed.astype(jnp.bfloat16)


def kernel(plan, tokens, gain_in, w_in_in, b_in_in, w_out_in, b_out_in, out, last, gain, w_in, b_in, w_out, b_out,
           gain_row, w_in_t, b_in_row, b_out_row,
           relay_far, relay_halo, ext0, ext1, far0, far1, sent1,
           far_send, far_recv, halo_send, halo_recv,
           pass_send, pass_recv, pass_halo_send, pass_halo_recv, load_sem):
    me = lax.axis_index("seq")
    chunk, near, halo, rows = plan.chunk, plan.near, plan.halo, plan.rows
    exts, fars = (ext0, ext1), (far0, far1)

    loads = [
        pltpu.make_async_copy(source, target, load_sem.at[at])
        for at, (source, target) in enumerate((
            (gain_in, gain_row), (w_in_in, w_in_t), (b_in_in, b_in_row), (w_out_in, w_out), (b_out_in, b_out_row),
            (tokens.at[pl.ds(0, near), :], ext0.at[:, pl.ds(halo, rows)]),
        ))
    ]
    for load in loads:
        load.start()

    barrier = pltpu.get_barrier_semaphore()
    for peer in plan.peers:
        pl.semaphore_signal(barrier, inc=1, device_id={"seq": lax.rem(me + peer, plan.count)}, device_id_type=MESH)
    pl.semaphore_wait(barrier, len(plan.peers))

    place = lax.rem(me, plan.plane) if plan.plane else me

    def along(hop):
        return {"seq": lax.rem(me + hop + plan.count, plan.count)}

    def far_copy(block, index, number, relay=None):
        cols = pl.ds(pl.multiple_of(number * chunk, LANES), chunk)
        if block == 0:
            source = tokens.at[pl.ds(near + index * TRACK_CH, TRACK_CH), cols]
        else:
            source = sent1.at[pl.ds(index * TRACK_CH, TRACK_CH), cols]
        if relay is None:
            target = fars[block].at[pl.ds(index * TRACK_CH, TRACK_CH), cols]
            arrived, hop = far_recv.at[block, index, number], plan.distances[index]
        else:
            target, arrived, hop = relay_far.at[block, :, cols], pass_recv.at[block, number], relay[2] - relay[1]
        return pltpu.make_async_remote_copy(
            src_ref=source, dst_ref=target, send_sem=far_send.at[block, index, number], recv_sem=arrived,
            device_id=along(hop), device_id_type=MESH,
        )

    def far_pass(block, relay, number):
        index, _, at, receiver = relay
        cols = pl.ds(pl.multiple_of(number * chunk, LANES), chunk)
        return pltpu.make_async_remote_copy(
            src_ref=relay_far.at[block, :, cols],
            dst_ref=fars[block].at[pl.ds(index * TRACK_CH, TRACK_CH), cols],
            send_sem=pass_send.at[block, number],
            recv_sem=far_recv.at[block, index, number],
            device_id=along(plan.plane + receiver - at), device_id_type=MESH,
        )

    def halo_copy(block, number, relay=None):
        first, height, from_end, width, _, _ = plan.pieces[number]
        where = (pl.ds(first, height), pl.ds(halo - from_end, width))
        if block == 0:
            source = tokens.at[pl.ds(first, height), pl.ds(rows - from_end, width)]
        else:
            source = ext1.at[pl.ds(first, height), pl.ds(halo + rows - from_end, width)]
        if relay is None:
            target, arrived, hop = exts[block].at[where], halo_recv.at[block, number], 1
        else:
            target, arrived = relay_halo.at[(block, *where)], pass_halo_recv.at[block, number]
            hop = relay[2] - relay[1]
        return pltpu.make_async_remote_copy(
            src_ref=source, dst_ref=target, send_sem=halo_send.at[block, number], recv_sem=arrived,
            device_id=along(hop), device_id_type=MESH,
        )

    def halo_pass(block, relay, number):
        first, height, from_end, width, _, _ = plan.pieces[number]
        where = (pl.ds(first, height), pl.ds(halo - from_end, width))
        return pltpu.make_async_remote_copy(
            src_ref=relay_halo.at[(block, *where)],
            dst_ref=exts[block].at[where],
            send_sem=pass_halo_send.at[block, number],
            recv_sem=halo_recv.at[block, number],
            device_id=along(plan.plane + relay[3] - relay[2]), device_id_type=MESH,
        )

    def start(make, key, *args, direct=True, relayed=True):
        relays = [relay for relay in plan.relays if relay[0] == key]
        if relayed:
            for relay in relays:
                @pl.when(place == relay[1])
                def _(relay=relay):
                    make(*args, relay=relay).start()

        if direct and relays:
            own = place >= 0
            for relay in relays:
                own = own & (place != relay[1])

            @pl.when(own)
            def _():
                make(*args).start()
        elif direct:
            make(*args).start()

    def send(block, step, **kinds):
        for index in reversed(range(plan.far)):
            start(far_copy, index, block, index, plan.chunks - 1 - step, **kinds)
        for piece, at in enumerate(plan.steps):
            @pl.when(step == at)
            def _(piece=piece):
                start(halo_copy, None, block, piece, **kinds)

    def pass_far(block, number):
        for relay in plan.relays:
            if relay[0] is not None:
                @pl.when(place == relay[2])
                def _(relay=relay):
                    far_copy(block, relay[0], number, relay).wait_recv()
                    far_pass(block, relay, number).start()

    def pass_halo(block, piece):
        for relay in plan.relays:
            if relay[0] is None:
                @pl.when(place == relay[2])
                def _(relay=relay):
                    halo_copy(block, piece, relay).wait_recv()
                    halo_pass(block, relay, piece).start()

    def hand_on(block, step):
        pass_far(block, plan.chunks - 1 - step)
        for piece, at in enumerate(plan.steps):
            @pl.when(step == at)
            def _(piece=piece):
                pass_halo(block, piece)

    def at_stage(block, step, lead, action, **kinds):
        for first, end, width in plan.stages:
            at = block * plan.chunks + step + width + lead
            for b in range(block, BLOCKS):
                low, high = max(first, b * plan.chunks), min(end, (b + 1) * plan.chunks)
                if low < high:
                    @pl.when(paced & (at >= low) & (at < high))
                    def _(b=b, at=at):
                        action(b, at - b * plan.chunks, **kinds)

    paced = me >= plan.count - plan.plane
    free = me < plan.count - plan.plane

    @pl.loop(0, plan.chunks + AHEAD)
    def _(step):
        @pl.when((step < plan.chunks) & free)
        def _():
            send(0, step)

        if plan.plane:
            width = plan.stages[0][2]

            @pl.when((step < width) & paced)
            def _():
                send(0, step, relayed=False)

            @pl.when((step < width + 1) & paced)
            def _():
                send(0, step, direct=False)

            @pl.when((step >= AHEAD) & (step - AHEAD < plan.chunks) & ((step - AHEAD < width) | free))
            def _():
                hand_on(0, step - AHEAD)

    for load in loads:
        load.wait()

    for block in range(BLOCKS):
        gain[block] = columns(gain_row[block:block + 1, :])
        b_in[block] = columns(b_in_row[block:block + 1, :])
        b_out[block] = columns(b_out_row[block:block + 1, :])
        w_in[block] = w_in_t[block].T

    def drain(block, number):
        for index in range(plan.far):
            far_copy(block, index, number).wait_send()
        for relay in plan.relays:
            if relay[0] is not None:
                @pl.when(place == relay[2])
                def _(relay=relay):
                    far_pass(block, relay, number).wait_send()

    def drain_halo(block):
        for piece in range(len(plan.pieces)):
            halo_copy(block, piece).wait_send()
            for relay in plan.relays:
                if relay[0] is None:
                    @pl.when(place == relay[2])
                    def _(relay=relay, piece=piece):
                        halo_pass(block, relay, piece).wait_send()

    for block in range(BLOCKS):
        ext, far = exts[block], fars[block]

        def advance(step, block=block, ext=ext, far=far, final=False):
            number = plan.chunks - 1 - step
            if plan.plane:
                ready = step - LAG + block * plan.chunks

                @pl.when(free & (ready >= 0) & (ready < plan.chunks))
                def _():
                    hand_on(1, ready)

            for index in range(plan.far):
                far_copy(block, index, number).wait_recv()
            for piece, (*_, reader) in enumerate(plan.pieces):
                @pl.when(number == reader)
                def _(piece=piece):
                    halo_copy(block, piece).wait_recv()

            if plan.plane:
                at_stage(block, step, 0, hand_on)
                at_stage(block, step, 0, send, relayed=False)
                at_stage(block, step, 1, send, direct=False)

            if final:
                last[...] = rotated_tile(plan, ext, far, 0).astype(jnp.bfloat16)
                return

            col = pl.multiple_of(number * chunk, LANES)
            value = mix_tile(
                rotated_tile(plan, ext, far, col),
                across(gain[block], chunk), w_in[block], across(b_in[block], chunk),
                w_out[block], across(b_out[block], chunk),
            )
            if block + 1 < BLOCKS:
                ext1[:, pl.ds(pl.multiple_of(halo + col, LANES), chunk)] = value[:near]
                sent1[:, pl.ds(col, chunk)] = value[near:]

                @pl.when(free)
                def _():
                    send(1, step)
            else:
                out[:, pl.ds(col, chunk)] = value
                drain(0, number)

                @pl.when(step == 0)
                def _():
                    drain_halo(0)

                @pl.when(step >= HELD)
                def _():
                    drain(1, number + HELD)

        if block + 1 < BLOCKS:
            pl.loop(0, plan.chunks)(advance)
        else:
            pl.loop(0, plan.chunks - 1)(advance)
            advance(plan.chunks - 1, final=True)

    drain(0, 0)
    pl.loop(0, min(HELD + 1, plan.chunks))(functools.partial(drain, 1))
    drain_halo(1)


def finish(chunk, done, last, gain, w_in, b_in, w_out, b_out, out, tail, sems):
    rest = pl.ds(chunk, done.shape[1] - chunk)
    body = pltpu.make_async_copy(done.at[:, rest], out.at[:, rest], sems.at[0])
    body.start()
    block = BLOCKS - 1
    tail[...] = mix_tile(
        last[...].astype(jnp.float32),
        across(gain[block], chunk), w_in[block], across(b_in[block], chunk),
        w_out[block], across(b_out[block], chunk),
    )
    end = pltpu.make_async_copy(tail, out.at[:, pl.ds(0, chunk)], sems.at[1])
    end.start()
    body.wait()
    end.wait()


def plane_of(mesh):
    devices = mesh.devices.reshape(-1)
    if mesh.shape["seq"] != devices.size or not hasattr(devices[0], "coords"):
        return 0
    places = [(*reversed(d.coords), d.core_on_chip) for d in devices]
    shape = tuple(max(p[axis] for p in places) + 1 for axis in range(4))
    plane = shape[1] * shape[2] * shape[3]
    ordered = [(i // plane, i // 4 % 2, i // 2 % 2, i % 2) for i in range(devices.size)]
    return plane if shape[1:] == (2, 2, 2) and shape[0] > 1 and places == ordered else 0


def solution(mesh):
    count = mesh.shape["seq"]
    plane = plane_of(mesh)

    def shards(tokens, norm_gain, in_weight, in_bias, out_weight, out_bias):
        channels, rows = tokens.shape
        plan = Plan(count, rows, min(CHUNK, rows // 2), plane)
        distant = plan.far * TRACK_CH
        wide = plan.halo + rows
        held = [
            pltpu.with_memory_space_constraint(x, pltpu.HBM)
            for x in (tokens, norm_gain, jnp.swapaxes(in_weight, 1, 2), in_bias, out_weight, out_bias)
        ]
        kept = pl.pallas_call(
            functools.partial(kernel, plan),
            out_shape=[
                pltpu.VMEM(tokens.shape, tokens.dtype),
                pltpu.VMEM((channels, plan.chunk), tokens.dtype),
                pltpu.VMEM((BLOCKS, channels, LANES), jnp.float32),
                pltpu.VMEM(in_weight.shape, jnp.bfloat16),
                pltpu.VMEM((BLOCKS, in_weight.shape[1], LANES), jnp.float32),
                pltpu.VMEM(out_weight.shape, jnp.bfloat16),
                pltpu.VMEM((BLOCKS, channels, LANES), jnp.float32),
            ],
            in_specs=[pl.BlockSpec(memory_space=pl.ANY)] * len(held),
            out_specs=[pl.BlockSpec(memory_space=pltpu.VMEM)] * 7,
            scratch_shapes=[
                *(pltpu.VMEM(held[at].shape, held[at].dtype) for at in (1, 2, 3, 5)),
                pltpu.VMEM((BLOCKS, TRACK_CH, rows), jnp.bfloat16),
                pltpu.VMEM((BLOCKS, plan.near, plan.halo), jnp.bfloat16),
                pltpu.VMEM((plan.near, wide), jnp.bfloat16),
                pltpu.VMEM((plan.near, wide), jnp.bfloat16),
                pltpu.VMEM((distant, rows), jnp.bfloat16),
                pltpu.VMEM((distant, rows), jnp.bfloat16),
                pltpu.VMEM((distant, rows), jnp.bfloat16),
                pltpu.SemaphoreType.DMA((BLOCKS, plan.far, plan.chunks)),
                pltpu.SemaphoreType.DMA((BLOCKS, plan.far, plan.chunks)),
                pltpu.SemaphoreType.DMA((BLOCKS, len(plan.pieces))),
                pltpu.SemaphoreType.DMA((BLOCKS, len(plan.pieces))),
                pltpu.SemaphoreType.DMA((BLOCKS, plan.chunks)),
                pltpu.SemaphoreType.DMA((BLOCKS, plan.chunks)),
                pltpu.SemaphoreType.DMA((BLOCKS, len(plan.pieces))),
                pltpu.SemaphoreType.DMA((BLOCKS, len(plan.pieces))),
                pltpu.SemaphoreType.DMA((len(held),)),
            ],
            compiler_params=pltpu.CompilerParams(
                collective_id=0, has_side_effects=True, vmem_limit_bytes=46 * 2**20
            ),
        )(*held)
        return pl.pallas_call(
            functools.partial(finish, plan.chunk),
            out_shape=jax.ShapeDtypeStruct(tokens.shape, tokens.dtype),
            in_specs=[pl.BlockSpec(memory_space=pltpu.VMEM)] * len(kept),
            out_specs=pl.BlockSpec(memory_space=pl.ANY),
            scratch_shapes=[
                pltpu.VMEM((channels, plan.chunk), tokens.dtype),
                pltpu.SemaphoreType.DMA((2,)),
            ],
            compiler_params=pltpu.CompilerParams(vmem_limit_bytes=14 * 2**20),
        )(*kept)

    return jax.shard_map(
        shards,
        mesh=mesh,
        in_specs=(P("batch", "seq"), P(), P(), P(), P(), P()),
        out_specs=P("batch", "seq"),
        check_vma=False,
    )
```

```python
import functools

import jax
import jax.numpy as jnp
from jax import lax
from jax.experimental import pallas as pl
from jax.experimental.pallas import tpu as pltpu
from jax.sharding import PartitionSpec as P

TRACK_CH = 16
TRACKS = 19
BLOCKS = 2
LANES = 128
CHUNK = 1024
LAG = 2
AHEAD = 1
HELD = 4
STAGES = ((0, 2), (4, 3), (8, 2))
MESH = pl.DeviceIdType.MESH


class Plan:
    def __init__(self, count, rows, chunk, plane):
        self.count, self.rows, self.chunk = count, rows, chunk
        self.chunks = rows // chunk
        self.short = 0
        while self.short + 1 < TRACKS and 2**self.short < rows:
            self.short += 1
        self.near = (1 + self.short) * TRACK_CH
        self.distances = [2 ** (t - 1) // rows for t in range(1 + self.short, TRACKS)]
        self.far = len(self.distances)
        self.halo = max(2 ** (self.short - 1), LANES)
        self.pieces = []
        small = sum(1 for t in range(1, 1 + self.short) if 2 ** (t - 1) < LANES)
        self.pieces.append((TRACK_CH, small * TRACK_CH, LANES, LANES, self.chunks - 1, 0))
        for t in range(1 + small, 1 + self.short):
            offset = 2 ** (t - 1)
            width = min(offset, chunk)
            for part in range(offset // width):
                from_end = offset - part * width
                source = (rows - from_end) // chunk
                self.pieces.append((t * TRACK_CH, TRACK_CH, from_end, width, source, part))
        self.pieces.sort(key=lambda piece: (piece[1] * piece[3] >= TRACK_CH * chunk, -piece[0], -piece[5], piece[2]))
        held, self.steps = 0, []
        for piece in self.pieces:
            self.steps.append(max(held // (TRACK_CH * chunk), self.chunks - 1 - piece[4]))
            held += piece[1] * piece[3]
        ends = [first for first, _ in STAGES[1:]] + [BLOCKS * self.chunks]
        self.stages = [(first, min(end, BLOCKS * self.chunks), width) for (first, width), end in zip(STAGES, ends)]
        self.plane = plane
        self.relays = []
        if plane:
            last = plane - 1
            self.relays = [(0, last, 2, 0), (None, last, 3, 0), (1, last - 1, 0, 0), (1, last, 1, 1)]
        peers = []
        hops = [1] + self.distances
        for _, sender, relay, receiver in self.relays:
            hops += [(relay - sender) % count, (plane + receiver - relay) % count]
        for d in hops:
            for signed in (d, count - d):
                if signed % count and signed % count not in peers:
                    peers.append(signed % count)
        self.peers = peers


def rotated_tile(plan, ext, far, col):
    tile, halo = plan.chunk, plan.halo
    parts = []
    for t in range(1 + plan.short):
        rows = pl.ds(t * TRACK_CH, TRACK_CH)
        offset = 0 if t == 0 else 2 ** (t - 1)
        if offset % LANES == 0:
            start = pl.multiple_of(halo - offset + col, LANES)
            parts.append(ext[rows, pl.ds(start, tile)].astype(jnp.float32))
        else:
            start = pl.multiple_of(halo - LANES + col, LANES)
            window = ext[rows, pl.ds(start, tile + LANES)].astype(jnp.float32)
            parts.append(pltpu.roll(window, offset, 1)[:, LANES:])
    parts.append(far[:, pl.ds(pl.multiple_of(col, LANES), tile)].astype(jnp.float32))
    return jnp.concatenate(parts, 0)


def columns(row):
    return jnp.broadcast_to(row, (LANES, row.shape[1])).T


def across(column, width):
    return jnp.concatenate([column] * (width // LANES), 1)


def mix_tile(as_float, gain, in_weight, in_bias, out_weight, out_bias):
    mean_square = jnp.mean(as_float * as_float, axis=0, keepdims=True)
    normed = (as_float * gain * lax.rsqrt(mean_square + 1e-06)).astype(jnp.bfloat16)
    pre_act = jnp.dot(in_weight, normed, preferred_element_type=jnp.float32) + in_bias
    inner = pre_act * (0.7978845608028654 + 0.035677408136300125 * (pre_act * pre_act))
    half = 0.5 * pre_act
    active = (half + half * jnp.tanh(inner)).astype(jnp.bfloat16)
    summed = as_float + jnp.dot(out_weight, active, preferred_element_type=jnp.float32) + out_bias
    return summed.astype(jnp.bfloat16)


def kernel(plan, tokens, gain_in, w_in_in, b_in_in, w_out_in, b_out_in, out, last, gain, w_in, b_in, w_out, b_out,
           gain_row, w_in_t, b_in_row, b_out_row,
           relay_far, relay_halo, ext0, ext1, far0, far1, sent1,
           far_send, far_recv, halo_send, halo_recv,
           pass_send, pass_recv, pass_halo_send, pass_halo_recv, load_sem):
    me = lax.axis_index("seq")
    chunk, near, halo, rows = plan.chunk, plan.near, plan.halo, plan.rows
    exts, fars = (ext0, ext1), (far0, far1)

    loads = [
        pltpu.make_async_copy(source, target, load_sem.at[at])
        for at, (source, target) in enumerate((
            (gain_in, gain_row), (w_in_in, w_in_t), (b_in_in, b_in_row), (w_out_in, w_out), (b_out_in, b_out_row),
            (tokens.at[pl.ds(0, near), :], ext0.at[:, pl.ds(halo, rows)]),
        ))
    ]
    for load in loads:
        load.start()

    barrier = pltpu.get_barrier_semaphore()
    for peer in plan.peers:
        pl.semaphore_signal(barrier, inc=1, device_id={"seq": lax.rem(me + peer, plan.count)}, device_id_type=MESH)
    pl.semaphore_wait(barrier, len(plan.peers))

    place = lax.rem(me, plan.plane) if plan.plane else me

    def along(hop):
        return {"seq": lax.rem(me + hop + plan.count, plan.count)}

    def far_copy(block, index, number, relay=None):
        cols = pl.ds(pl.multiple_of(number * chunk, LANES), chunk)
        if block == 0:
            source = tokens.at[pl.ds(near + index * TRACK_CH, TRACK_CH), cols]
        else:
            source = sent1.at[pl.ds(index * TRACK_CH, TRACK_CH), cols]
        if relay is None:
            target = fars[block].at[pl.ds(index * TRACK_CH, TRACK_CH), cols]
            arrived, hop = far_recv.at[block, index, number], plan.distances[index]
        else:
            target, arrived, hop = relay_far.at[block, :, cols], pass_recv.at[block, number], relay[2] - relay[1]
        return pltpu.make_async_remote_copy(
            src_ref=source, dst_ref=target, send_sem=far_send.at[block, index, number], recv_sem=arrived,
            device_id=along(hop), device_id_type=MESH,
        )

    def far_pass(block, relay, number):
        index, _, at, receiver = relay
        cols = pl.ds(pl.multiple_of(number * chunk, LANES), chunk)
        return pltpu.make_async_remote_copy(
            src_ref=relay_far.at[block, :, cols],
            dst_ref=fars[block].at[pl.ds(index * TRACK_CH, TRACK_CH), cols],
            send_sem=pass_send.at[block, number],
            recv_sem=far_recv.at[block, index, number],
            device_id=along(plan.plane + receiver - at), device_id_type=MESH,
        )

    def halo_copy(block, number, relay=None):
        first, height, from_end, width, _, _ = plan.pieces[number]
        where = (pl.ds(first, height), pl.ds(halo - from_end, width))
        if block == 0:
            source = tokens.at[pl.ds(first, height), pl.ds(rows - from_end, width)]
        else:
            source = ext1.at[pl.ds(first, height), pl.ds(halo + rows - from_end, width)]
        if relay is None:
            target, arrived, hop = exts[block].at[where], halo_recv.at[block, number], 1
        else:
            target, arrived = relay_halo.at[(block, *where)], pass_halo_recv.at[block, number]
            hop = relay[2] - relay[1]
        return pltpu.make_async_remote_copy(
            src_ref=source, dst_ref=target, send_sem=halo_send.at[block, number], recv_sem=arrived,
            device_id=along(hop), device_id_type=MESH,
        )

    def halo_pass(block, relay, number):
        first, height, from_end, width, _, _ = plan.pieces[number]
        where = (pl.ds(first, height), pl.ds(halo - from_end, width))
        return pltpu.make_async_remote_copy(
            src_ref=relay_halo.at[(block, *where)],
            dst_ref=exts[block].at[where],
            send_sem=pass_halo_send.at[block, number],
            recv_sem=halo_recv.at[block, number],
            device_id=along(plan.plane + relay[3] - relay[2]), device_id_type=MESH,
        )

    def start(make, key, *args, direct=True, relayed=True):
        relays = [relay for relay in plan.relays if relay[0] == key]
        if relayed:
            for relay in relays:
                @pl.when(place == relay[1])
                def _(relay=relay):
                    make(*args, relay=relay).start()

        if direct and relays:
            own = place >= 0
            for relay in relays:
                own = own & (place != relay[1])

            @pl.when(own)
            def _():
                make(*args).start()
        elif direct:
            make(*args).start()

    def send(block, step, **kinds):
        for index in reversed(range(plan.far)):
            start(far_copy, index, block, index, plan.chunks - 1 - step, **kinds)
        for piece, at in enumerate(plan.steps):
            @pl.when(step == at)
            def _(piece=piece):
                start(halo_copy, None, block, piece, **kinds)

    def pass_far(block, number):
        for relay in plan.relays:
            if relay[0] is not None:
                @pl.when(place == relay[2])
                def _(relay=relay):
                    far_copy(block, relay[0], number, relay).wait_recv()
                    far_pass(block, relay, number).start()

    def pass_halo(block, piece):
        for relay in plan.relays:
            if relay[0] is None:
                @pl.when(place == relay[2])
                def _(relay=relay):
                    halo_copy(block, piece, relay).wait_recv()
                    halo_pass(block, relay, piece).start()

    def hand_on(block, step):
        pass_far(block, plan.chunks - 1 - step)
        for piece, at in enumerate(plan.steps):
            @pl.when(step == at)
            def _(piece=piece):
                pass_halo(block, piece)

    def at_stage(block, step, lead, action, **kinds):
        for first, end, width in plan.stages:
            at = block * plan.chunks + step + width + lead
            for b in range(block, BLOCKS):
                low, high = max(first, b * plan.chunks), min(end, (b + 1) * plan.chunks)
                if low < high:
                    @pl.when(paced & (at >= low) & (at < high))
                    def _(b=b, at=at):
                        action(b, at - b * plan.chunks, **kinds)

    paced = me >= plan.count - plan.plane
    free = me < plan.count - plan.plane

    @pl.loop(0, plan.chunks + AHEAD)
    def _(step):
        @pl.when((step < plan.chunks) & free)
        def _():
            send(0, step)

        if plan.plane:
            width = plan.stages[0][2]

            @pl.when((step < width) & paced)
            def _():
                send(0, step, relayed=False)

            @pl.when((step < width + 1) & paced)
            def _():
                send(0, step, direct=False)

            @pl.when((step >= AHEAD) & (step - AHEAD < plan.chunks) & ((step - AHEAD < width) | free))
            def _():
                hand_on(0, step - AHEAD)

    for load in loads:
        load.wait()

    for block in range(BLOCKS):
        gain[block] = columns(gain_row[block:block + 1, :])
        b_in[block] = columns(b_in_row[block:block + 1, :])
        b_out[block] = columns(b_out_row[block:block + 1, :])
        w_in[block] = w_in_t[block].T

    def drain(block, number):
        for index in range(plan.far):
            far_copy(block, index, number).wait_send()
        for relay in plan.relays:
            if relay[0] is not None:
                @pl.when(place == relay[2])
                def _(relay=relay):
                    far_pass(block, relay, number).wait_send()

    def drain_halo(block):
        for piece in range(len(plan.pieces)):
            halo_copy(block, piece).wait_send()
            for relay in plan.relays:
                if relay[0] is None:
                    @pl.when(place == relay[2])
                    def _(relay=relay, piece=piece):
                        halo_pass(block, relay, piece).wait_send()

    for block in range(BLOCKS):
        ext, far = exts[block], fars[block]

        def advance(step, block=block, ext=ext, far=far, final=False):
            number = plan.chunks - 1 - step
            if plan.plane:
                ready = step - LAG + block * plan.chunks

                @pl.when(free & (ready >= 0) & (ready < plan.chunks))
                def _():
                    hand_on(1, ready)

            for index in range(plan.far):
                far_copy(block, index, number).wait_recv()
            for piece, (*_, reader) in enumerate(plan.pieces):
                @pl.when(number == reader)
                def _(piece=piece):
                    halo_copy(block, piece).wait_recv()

            if plan.plane:
                at_stage(block, step, 0, hand_on)
                at_stage(block, step, 0, send, relayed=False)
                at_stage(block, step, 1, send, direct=False)

            if final:
                last[...] = rotated_tile(plan, ext, far, 0).astype(jnp.bfloat16)
                return

            col = pl.multiple_of(number * chunk, LANES)
            value = mix_tile(
                rotated_tile(plan, ext, far, col),
                across(gain[block], chunk), w_in[block], across(b_in[block], chunk),
                w_out[block], across(b_out[block], chunk),
            )
            if block + 1 < BLOCKS:
                ext1[:, pl.ds(pl.multiple_of(halo + col, LANES), chunk)] = value[:near]
                sent1[:, pl.ds(col, chunk)] = value[near:]

                @pl.when(free)
                def _():
                    send(1, step)
            else:
                out[:, pl.ds(col, chunk)] = value
                drain(0, number)

                @pl.when(step == 0)
                def _():
                    drain_halo(0)

                @pl.when(step >= HELD)
                def _():
                    drain(1, number + HELD)

        if block + 1 < BLOCKS:
            pl.loop(0, plan.chunks)(advance)
        else:
            pl.loop(0, plan.chunks - 1)(advance)
            advance(plan.chunks - 1, final=True)

    drain(0, 0)
    pl.loop(0, min(HELD + 1, plan.chunks))(functools.partial(drain, 1))
    drain_halo(1)


def finish(chunk, done, last, gain, w_in, b_in, w_out, b_out, out, tail, sems):
    rest = pl.ds(chunk, done.shape[1] - chunk)
    body = pltpu.make_async_copy(done.at[:, rest], out.at[:, rest], sems.at[0])
    body.start()
    block = BLOCKS - 1
    tail[...] = mix_tile(
        last[...].astype(jnp.float32),
        across(gain[block], chunk), w_in[block], across(b_in[block], chunk),
        w_out[block], across(b_out[block], chunk),
    )
    end = pltpu.make_async_copy(tail, out.at[:, pl.ds(0, chunk)], sems.at[1])
    end.start()
    body.wait()
    end.wait()


def plane_of(mesh):
    devices = mesh.devices.reshape(-1)
    if mesh.shape["seq"] != devices.size or not hasattr(devices[0], "coords"):
        return 0
    places = [(*reversed(d.coords), d.core_on_chip) for d in devices]
    shape = tuple(max(p[axis] for p in places) + 1 for axis in range(4))
    plane = shape[1] * shape[2] * shape[3]
    ordered = [(i // plane, i // 4 % 2, i // 2 % 2, i % 2) for i in range(devices.size)]
    return plane if shape[1:] == (2, 2, 2) and shape[0] > 1 and places == ordered else 0


def solution(mesh):
    count = mesh.shape["seq"]
    plane = plane_of(mesh)

    def shards(tokens, norm_gain, in_weight, in_bias, out_weight, out_bias):
        channels, rows = tokens.shape
        plan = Plan(count, rows, min(CHUNK, rows // 2), plane)
        distant = plan.far * TRACK_CH
        wide = plan.halo + rows
        held = [
            pltpu.with_memory_space_constraint(x, pltpu.HBM)
            for x in (tokens, norm_gain, jnp.swapaxes(in_weight, 1, 2), in_bias, out_weight, out_bias)
        ]
        kept = pl.pallas_call(
            functools.partial(kernel, plan),
            out_shape=[
                pltpu.VMEM(tokens.shape, tokens.dtype),
                pltpu.VMEM((channels, plan.chunk), tokens.dtype),
                pltpu.VMEM((BLOCKS, channels, LANES), jnp.float32),
                pltpu.VMEM(in_weight.shape, jnp.bfloat16),
                pltpu.VMEM((BLOCKS, in_weight.shape[1], LANES), jnp.float32),
                pltpu.VMEM(out_weight.shape, jnp.bfloat16),
                pltpu.VMEM((BLOCKS, channels, LANES), jnp.float32),
            ],
            in_specs=[pl.BlockSpec(memory_space=pl.ANY)] * len(held),
            out_specs=[pl.BlockSpec(memory_space=pltpu.VMEM)] * 7,
            scratch_shapes=[
                *(pltpu.VMEM(held[at].shape, held[at].dtype) for at in (1, 2, 3, 5)),
                pltpu.VMEM((BLOCKS, TRACK_CH, rows), jnp.bfloat16),
                pltpu.VMEM((BLOCKS, plan.near, plan.halo), jnp.bfloat16),
                pltpu.VMEM((plan.near, wide), jnp.bfloat16),
                pltpu.VMEM((plan.near, wide), jnp.bfloat16),
                pltpu.VMEM((distant, rows), jnp.bfloat16),
                pltpu.VMEM((distant, rows), jnp.bfloat16),
                pltpu.VMEM((distant, rows), jnp.bfloat16),
                pltpu.SemaphoreType.DMA((BLOCKS, plan.far, plan.chunks)),
                pltpu.SemaphoreType.DMA((BLOCKS, plan.far, plan.chunks)),
                pltpu.SemaphoreType.DMA((BLOCKS, len(plan.pieces))),
                pltpu.SemaphoreType.DMA((BLOCKS, len(plan.pieces))),
                pltpu.SemaphoreType.DMA((BLOCKS, plan.chunks)),
                pltpu.SemaphoreType.DMA((BLOCKS, plan.chunks)),
                pltpu.SemaphoreType.DMA((BLOCKS, len(plan.pieces))),
                pltpu.SemaphoreType.DMA((BLOCKS, len(plan.pieces))),
                pltpu.SemaphoreType.DMA((len(held),)),
            ],
            compiler_params=pltpu.CompilerParams(
                collective_id=0, has_side_effects=True, vmem_limit_bytes=46 * 2**20
            ),
        )(*held)
        return pl.pallas_call(
            functools.partial(finish, plan.chunk),
            out_shape=jax.ShapeDtypeStruct(tokens.shape, tokens.dtype),
            in_specs=[pl.BlockSpec(memory_space=pltpu.VMEM)] * len(kept),
            out_specs=pl.BlockSpec(memory_space=pl.ANY),
            scratch_shapes=[
                pltpu.VMEM((channels, plan.chunk), tokens.dtype),
                pltpu.SemaphoreType.DMA((2,)),
            ],
            compiler_params=pltpu.CompilerParams(vmem_limit_bytes=14 * 2**20),
        )(*kept)

    return jax.shard_map(
        shards,
        mesh=mesh,
        in_specs=(P("batch", "seq"), P(), P(), P(), P(), P()),
        out_specs=P("batch", "seq"),
        check_vma=False,
    )
```
